128 devices in a mesh: seq: 16 (over z_lo, x, core), res: 8 (over y, z_hi).
Axes of the slice: x: 4, y: 4, z: 4 (z_hi: 2, z_lo: 2; z = z_hi * 2 + z_lo), core: 2. Of those that a mesh axis runs over, the one named last changes fastest.
Arguments:
- states: bfloat16 [512, 256, 768], P('seq', 'res'), may hold values from -6 to 6
- row_query: bfloat16 [768, 768], replicated, as said below
- row_key: bfloat16 [768, 768], replicated
- row_value: bfloat16 [768, 768], replicated, may hold values from -0.21875 to 0.21875
- row_out: bfloat16 [768, 768], replicated, may hold values from -0.21875 to 0.21875
- col_query: bfloat16 [768, 768], replicated, as said below
- col_key: bfloat16 [768, 768], replicated
- col_value: bfloat16 [768, 768], replicated, may hold values from -0.21875 to 0.21875
- col_out: bfloat16 [768, 768], replicated, may hold values from -0.21875 to 0.21875
Outputs:
- updated: bfloat16 [512, 256, 768], P('seq', 'res')
The draws below stay inside these ranges and needn't reach their ends.
Inputs may be any that keep to these rules, and one draw needn't show every extreme that they name: No bound on the size of row_query and row_key entries or of the scores they give is promised. No bound on the size of col_query and col_key entries or of the scores they give is promised.
All inputs are finite; a program needn't handle non-finite values.
Results may differ from the reference program's by a relative error of at most 0.02.
Values may be sent and summed in bfloat16 or wider, within the bound.
A program may use at most 128 MiB of HBM per device.

```python
import math
import jax
import jax.numpy as jnp
from jax import lax

D = 768
HEADS = 12
ROWS = 512
COLS = 256


def query_pair(key, tag):
    base = jax.random.fold_in(key, tag)
    keys_part = jax.random.normal(jax.random.fold_in(base, 1), (D, D), jnp.float32) * D ** (-0.5)
    query_part = jax.random.normal(jax.random.fold_in(base, 2), (D, D), jnp.float32) * 2.0 * D ** (-0.5)
    return (query_part, keys_part)


def draw_row_query(key, part):
    return query_pair(key, 101)[0].astype(jnp.bfloat16)


def draw_row_key(key, part):
    return query_pair(key, 101)[1].astype(jnp.bfloat16)


def draw_col_query(key, part):
    return query_pair(key, 202)[0].astype(jnp.bfloat16)


def draw_col_key(key, part):
    return query_pair(key, 202)[1].astype(jnp.bfloat16)


def levels(stream_key, shape, pieces, low, top_value):
    def one(axis_at, blocks):
        steps = jax.random.uniform(jax.random.fold_in(jax.random.fold_in(stream_key, 6), axis_at), (blocks,), jnp.float32, low / len(pieces), top_value / len(pieces))
        return jnp.repeat(jnp.exp(steps), shape[axis_at] // blocks).reshape((-1,) + (1,) * (len(shape) - axis_at - 1))

    level = one(*pieces[0])
    for cut in pieces[1:]:
        level = level * one(*cut)
    return level


def centred(own_key, dims, scale, reach, shards=(), kind=jnp.bfloat16):
    entries = jax.random.normal(own_key, dims, jnp.float32) * scale
    if len(shards) > 0:
        entries = levels(own_key, dims, shards, -0.22, 0.18) * entries
    return jnp.clip(entries, min=-reach, max=reach).astype(kind)


def setup_inputs(seed: int = 0) -> dict:
    splits = jax.random.split(jax.random.key(seed), 10)
    states = centred(splits[0], (ROWS, COLS, D), 1.0, 6.0, ((0, 16), (1, 8)))
    row_query = draw_row_query(jax.random.fold_in(splits[9], 71), 0)
    row_key = draw_row_key(jax.random.fold_in(splits[9], 71), 0)
    row_value = centred(splits[3], (D, D), D ** -0.5, 0.21875)
    row_out = centred(splits[4], (D, D), D ** -0.5, 0.21875)
    col_query = draw_col_query(jax.random.fold_in(splits[9], 71), 0)
    col_key = draw_col_key(jax.random.fold_in(splits[9], 71), 0)
    col_value = centred(splits[7], (D, D), D ** -0.5, 0.21875)
    col_out = centred(splits[8], (D, D), D ** -0.5, 0.21875)
    return {"states": states, "row_query": row_query, "row_key": row_key, "row_value": row_value, "row_out": row_out, "col_query": col_query, "col_key": col_key, "col_value": col_value, "col_out": col_out}


def normalize(states):
    values = states.astype(jnp.float32)
    center = values - lax.optimization_barrier(jnp.mean(values, axis=-1, keepdims=True))
    spread = lax.optimization_barrier(jnp.mean(center * center, axis=-1, keepdims=True))
    return (center * lax.rsqrt(spread + 1e-05)).astype(jnp.bfloat16)

def project(inputs, weight):
    flat = inputs.reshape(-1, inputs.shape[-1])
    result = jnp.dot(flat, weight, preferred_element_type=jnp.float32)
    return result.reshape(inputs.shape[:-1] + (weight.shape[1],))

def reference(states, row_query, row_key, row_value, row_out, col_query, col_key, col_value, col_out):
    nrows, ncols = (states.shape[0], states.shape[1])
    head_dim = D // HEADS
    normed = normalize(states)
    q1 = project(normed, row_query).astype(jnp.bfloat16).reshape(nrows, ncols, HEADS, head_dim)
    k1 = project(normed, row_key).astype(jnp.bfloat16).reshape(nrows, ncols, HEADS, head_dim)
    v1 = project(normed, row_value).astype(jnp.bfloat16).reshape(nrows, ncols, HEADS, head_dim)
    tied = jnp.einsum('rihd,rjhd->hij', q1.astype(jnp.float32), k1.astype(jnp.float32))
    tied = tied * (head_dim ** (-0.5) / math.sqrt(nrows))
    prob1 = jax.nn.softmax(tied, axis=-1).astype(jnp.bfloat16)
    o1 = jnp.einsum('hij,rjhd->rihd', prob1.astype(jnp.float32), v1.astype(jnp.float32)).astype(jnp.bfloat16)
    mid = (states.astype(jnp.float32) + project(o1.reshape(nrows, ncols, D), row_out)).astype(jnp.bfloat16)
    normed2 = normalize(mid)
    q2 = project(normed2, col_query).astype(jnp.bfloat16)
    k2 = project(normed2, col_key).astype(jnp.bfloat16)
    v2 = project(normed2, col_value).astype(jnp.bfloat16)
    block = math.gcd(ncols, 8)

    def arrange(field):
        field = field.reshape(nrows, ncols, HEADS, head_dim).transpose(1, 0, 2, 3)
        return field.reshape(ncols // block, block, nrows, HEADS, head_dim)

    def attend(triple):
        qb, kb, vb = triple
        score = jnp.einsum('crhd,cshd->chrs', qb.astype(jnp.float32), kb.astype(jnp.float32)) * head_dim ** (-0.5)
        prob2 = jax.nn.softmax(score, axis=-1).astype(jnp.bfloat16)
        return jnp.einsum('chrs,cshd->crhd', prob2.astype(jnp.float32), vb.astype(jnp.float32)).astype(jnp.bfloat16)
    o2 = lax.map(attend, (arrange(q2), arrange(k2), arrange(v2)))
    o2 = o2.reshape(ncols, nrows, D).transpose(1, 0, 2)
    colupd = project(o2, col_out).astype(jnp.bfloat16)
    colupd = lax.optimization_barrier(colupd)
    return (mid.astype(jnp.float32) + colupd.astype(jnp.float32)).astype(jnp.bfloat16)
```

```python
import math

import jax
import jax.numpy as jnp
from jax import lax
from jax.sharding import PartitionSpec as P

D = 768
HEADS = 12
HD = D // HEADS


def normalize(states):
    values = states.astype(jnp.float32)
    center = values - jnp.mean(values, axis=-1, keepdims=True)
    spread = jnp.mean(center * center, axis=-1, keepdims=True)
    return (center * lax.rsqrt(spread + 1e-05)).astype(jnp.bfloat16)


def project(inputs, weight):
    return jnp.dot(inputs, weight, preferred_element_type=jnp.float32)


def on_device(
    states, row_query, row_key, row_value, row_out, col_query, col_key, col_value, col_out
):
    rows, cols = states.shape[0], states.shape[1]
    seq, res = lax.axis_size("seq"), lax.axis_size("res")
    own_rows, own_cols = rows // res, cols // seq
    all_rows, all_cols = rows * seq, cols * res
    tied_scale = HD ** (-0.5) / math.sqrt(all_rows)
    moved = lax.all_to_all(
        states.reshape(res, own_rows, cols, D), "res", split_axis=0, concat_axis=0
    )
    by_row = moved.transpose(1, 0, 2, 3).reshape(own_rows, all_cols, D)
    normed = normalize(by_row)
    q1 = project(normed, row_query).astype(jnp.bfloat16).reshape(own_rows, all_cols, HEADS, HD)
    k1 = project(normed, row_key).astype(jnp.bfloat16).reshape(own_rows, all_cols, HEADS, HD)
    v1 = project(normed, row_value).astype(jnp.bfloat16).reshape(own_rows, all_cols, HEADS, HD)
    part = jnp.einsum("rihd,rjhd->hij", q1, k1, preferred_element_type=jnp.float32) * tied_scale
    part = part.reshape(HEADS * all_cols, all_cols)
    tied = lax.psum_scatter(part, ("seq", "res"), scatter_dimension=0, tiled=True)
    prob1 = jax.nn.softmax(tied, axis=-1).astype(jnp.bfloat16)
    prob1 = lax.all_gather(prob1, ("seq", "res"), axis=0, tiled=True)
    prob1 = prob1.reshape(HEADS, all_cols, all_cols)
    o1 = jnp.einsum("hij,rjhd->rihd", prob1, v1, preferred_element_type=jnp.float32)
    o1 = o1.astype(jnp.bfloat16).reshape(own_rows, all_cols, D)
    mid = (by_row.astype(jnp.float32) + project(o1, row_out)).astype(jnp.bfloat16)
    mid = mid.reshape(own_rows, res, seq, own_cols, D).transpose(2, 1, 0, 3, 4)
    mid = mid.reshape(seq * res, own_rows, own_cols, D)
    mid = lax.all_to_all(mid, ("seq", "res"), split_axis=0, concat_axis=0)
    mid = mid.reshape(all_rows, own_cols, D).transpose(1, 0, 2)
    normed2 = normalize(mid)
    q2 = project(normed2, col_query).astype(jnp.bfloat16).reshape(own_cols, all_rows, HEADS, HD)
    k2 = project(normed2, col_key).astype(jnp.bfloat16).reshape(own_cols, all_rows, HEADS, HD)
    v2 = project(normed2, col_value).astype(jnp.bfloat16).reshape(own_cols, all_rows, HEADS, HD)
    score = jnp.einsum("crhd,cshd->chrs", q2, k2, preferred_element_type=jnp.float32)
    prob2 = jax.nn.softmax(score * HD ** (-0.5), axis=-1).astype(jnp.bfloat16)
    o2 = jnp.einsum("chrs,cshd->crhd", prob2, v2, preferred_element_type=jnp.float32)
    o2 = o2.astype(jnp.bfloat16).reshape(own_cols, all_rows, D)
    colupd = project(o2, col_out).astype(jnp.bfloat16)
    updated = (mid.astype(jnp.float32) + colupd.astype(jnp.float32)).astype(jnp.bfloat16)
    updated = updated.reshape(own_cols, seq, rows, D).transpose(1, 2, 0, 3)
    updated = lax.all_to_all(updated, "seq", split_axis=0, concat_axis=0)
    return updated.transpose(1, 0, 2, 3).reshape(rows, cols, D)


def solution(mesh):
    placed = (P("seq", "res", None), P(), P(), P(), P(), P(), P(), P(), P())
    return jax.shard_map(
        on_device, mesh=mesh, in_specs=placed, out_specs=P("seq", "res", None), check_vma=False
    )
```

```python
import functools
import math

import jax
import jax.numpy as jnp
from jax import lax
from jax.experimental import pallas as pl
from jax.experimental.pallas import tpu as pltpu
from jax.sharding import PartitionSpec as P

D = 768
HEADS = 12
HD = D // HEADS
MESH = pl.DeviceIdType.MESH


def normalize(states):
    values = states.astype(jnp.float32)
    center = values - jnp.mean(values, axis=-1, keepdims=True)
    spread = jnp.mean(center * center, axis=-1, keepdims=True)
    return (center * lax.rsqrt(spread + 1e-05)).astype(jnp.bfloat16)


def project(inputs, weight):
    return jnp.dot(inputs, weight, preferred_element_type=jnp.float32)


def tied_softmax_kernel(scale, part, prob, pair_in, pair_sum, chunk_in, chunk_out,
                        pair_send, pair_recv, chunk_send, chunk_recv,
                        prob_send, prob_recv, half_send, half_recv):
    seq, res = lax.axis_index("seq"), lax.axis_index("res")
    core, me = seq % 2, (seq // 2) * 8 + res
    partner = {"seq": seq + 1 - 2 * core, "res": res}
    mine, other = 6 * core, 6 * (1 - core)

    def chip(m):
        return {"seq": 2 * (m // 8) + core, "res": m % 8}

    barrier = pltpu.get_barrier_semaphore()

    @pl.loop(1, 64)
    def _(k):
        pl.semaphore_signal(barrier, inc=1, device_id=chip((me + k) % 64), device_id_type=MESH)

    pl.semaphore_signal(barrier, inc=1, device_id=partner, device_id_type=MESH)
    pl.semaphore_wait(barrier, 64)

    def pair_copy(h):
        return pltpu.make_async_remote_copy(
            src_ref=part.at[other + h], dst_ref=pair_in.at[h], send_sem=pair_send.at[h],
            recv_sem=pair_recv.at[h], device_id=partner, device_id_type=MESH)

    def chunk_copy(m, slot):
        return pltpu.make_async_remote_copy(
            src_ref=pair_sum.at[pl.ds(3 * (m // 32), 3), m % 32], dst_ref=chunk_in.at[slot],
            send_sem=chunk_send.at[m], recv_sem=chunk_recv.at[slot],
            device_id=chip(m), device_id_type=MESH)

    def prob_copy(m, owner):
        return pltpu.make_async_remote_copy(
            src_ref=chunk_out, dst_ref=prob.at[pl.ds(mine + 3 * (owner // 32), 3), owner % 32],
            send_sem=prob_send.at[m], recv_sem=prob_recv.at[owner],
            device_id=chip(m), device_id_type=MESH)

    @pl.loop(0, 6)
    def _(h):
        pair_copy(h).start()

    @pl.loop(0, 6)
    def _(h):
        pair_copy(h).wait_recv()
        pair_sum[h] = part[mine + h] + pair_in[h]

    @pl.loop(1, 64)
    def _(k):
        chunk_copy((me + k) % 64, me).start()

    def add(k, total):
        source = (me + k) % 64
        chunk_copy(source, source).wait_recv()
        return total + chunk_in[source]

    total = lax.fori_loop(1, 64, add, pair_sum[pl.ds(3 * (me // 32), 3), me % 32]) * scale
    total = jnp.exp(total - jnp.max(total, axis=-1, keepdims=True))
    total = (total / jnp.sum(total, axis=-1, keepdims=True)).astype(jnp.bfloat16)
    chunk_out[...] = total
    prob[pl.ds(mine + 3 * (me // 32), 3), me % 32] = total

    @pl.loop(1, 64)
    def _(k):
        prob_copy((me + k) % 64, me).start()

    @pl.loop(1, 64)
    def _(k):
        source = (me + k) % 64
        prob_copy(source, source).wait_recv()

    def half_copy(base):
        return pltpu.make_async_remote_copy(
            src_ref=prob.at[pl.ds(mine, 6)], dst_ref=prob.at[pl.ds(base, 6)],
            send_sem=half_send, recv_sem=half_recv, device_id=partner, device_id_type=MESH)

    half_copy(mine).start()
    half_copy(other).wait_recv()

    @pl.loop(1, 64)
    def _(k):
        source = (me + k) % 64
        chunk_copy(source, me).wait_send()
        prob_copy(source, me).wait_send()

    @pl.loop(0, 6)
    def _(h):
        pair_copy(h).wait_send()

    half_copy(mine).wait_send()


def tied_softmax(part, scale):
    dma = pltpu.SemaphoreType.DMA
    return pl.pallas_call(
        functools.partial(tied_softmax_kernel, scale),
        out_shape=jax.ShapeDtypeStruct((12, 32, 8, 256), jnp.bfloat16),
        in_specs=[pl.BlockSpec(memory_space=pltpu.VMEM)],
        out_specs=pl.BlockSpec(memory_space=pltpu.VMEM),
        scratch_shapes=[
            pltpu.VMEM((6, 32, 8, 256), jnp.float32),
            pltpu.VMEM((6, 32, 8, 256), jnp.float32),
            pltpu.VMEM((64, 3, 8, 256), jnp.float32),
            pltpu.VMEM((3, 8, 256), jnp.bfloat16),
            dma((6,)), dma((6,)), dma((64,)), dma((64,)), dma((64,)), dma((64,)), dma, dma,
        ],
        compiler_params=pltpu.CompilerParams(collective_id=0, has_side_effects=True),
    )(part)


def on_device(
    states, row_query, row_key, row_value, row_out, col_query, col_key, col_value, col_out
):
    rows, cols = states.shape[0], states.shape[1]
    seq, res = lax.axis_size("seq"), lax.axis_size("res")
    own_rows, own_cols = rows // res, cols // seq
    all_rows, all_cols = rows * seq, cols * res
    tied_scale = HD ** (-0.5) / math.sqrt(all_rows)
    moved = lax.all_to_all(
        states.reshape(res, own_rows, cols, D), "res", split_axis=0, concat_axis=0
    )
    by_row = moved.transpose(1, 0, 2, 3).reshape(own_rows, all_cols, D)
    normed = normalize(by_row)
    q1 = project(normed, row_query).astype(jnp.bfloat16).reshape(own_rows, all_cols, HEADS, HD)
    k1 = project(normed, row_key).astype(jnp.bfloat16).reshape(own_rows, all_cols, HEADS, HD)
    v1 = project(normed, row_value).astype(jnp.bfloat16).reshape(own_rows, all_cols, HEADS, HD)
    part = jnp.einsum("rihd,rjhd->hij", q1, k1, preferred_element_type=jnp.float32)
    part = part.reshape(HEADS, 32, 8, all_cols)
    prob1 = tied_softmax(part, tied_scale)
    prob1 = prob1.reshape(HEADS, all_cols, all_cols)
    o1 = jnp.einsum("hij,rjhd->rihd", prob1, v1, preferred_element_type=jnp.float32)
    o1 = o1.astype(jnp.bfloat16).reshape(own_rows, all_cols, D)
    mid = (by_row.astype(jnp.float32) + project(o1, row_out)).astype(jnp.bfloat16)
    mid = mid.reshape(own_rows, res, seq, own_cols, D).transpose(2, 1, 0, 3, 4)
    mid = mid.reshape(seq * res, own_rows, own_cols, D)
    mid = lax.all_to_all(mid, ("seq", "res"), split_axis=0, concat_axis=0)
    mid = mid.reshape(all_rows, own_cols, D).transpose(1, 0, 2)
    normed2 = normalize(mid)
    q2 = project(normed2, col_query).astype(jnp.bfloat16).reshape(own_cols, all_rows, HEADS, HD)
    k2 = project(normed2, col_key).astype(jnp.bfloat16).reshape(own_cols, all_rows, HEADS, HD)
    v2 = project(normed2, col_value).astype(jnp.bfloat16).reshape(own_cols, all_rows, HEADS, HD)
    score = jnp.einsum("crhd,cshd->chrs", q2, k2, preferred_element_type=jnp.float32)
    prob2 = jax.nn.softmax(score * HD ** (-0.5), axis=-1).astype(jnp.bfloat16)
    o2 = jnp.einsum("chrs,cshd->crhd", prob2, v2, preferred_element_type=jnp.float32)
    o2 = o2.astype(jnp.bfloat16).reshape(own_cols, all_rows, D)
    colupd = project(o2, col_out).astype(jnp.bfloat16)
    updated = (mid.astype(jnp.float32) + colupd.astype(jnp.float32)).astype(jnp.bfloat16)
    updated = updated.reshape(own_cols, seq, rows, D).transpose(1, 2, 0, 3)
    updated = lax.all_to_all(updated, "seq", split_axis=0, concat_axis=0)
    return updated.transpose(1, 0, 2, 3).reshape(rows, cols, D)


def solution(mesh):
    placed = (P("seq", "res", None), P(), P(), P(), P(), P(), P(), P(), P())
    return jax.shard_map(
        on_device, mesh=mesh, in_specs=placed, out_specs=P("seq", "res", None), check_vma=False
    )
```
